32 devices in a mesh: tm: 16 (over z, x, core), head: 2 (over y).
Axes of the slice: x: 2, y: 2, z: 4, core: 2. Of those that a mesh axis runs over, the one named last changes fastest.
Arguments:
- queries: bfloat16 [16, 392, 1024], P('tm', None, 'head'), may hold values from -6 to 6
- key_tokens: bfloat16 [16, 392, 1024], P('tm', None, 'head'), may hold values from -6 to 6
- value_tokens: bfloat16 [16, 392, 1024], P('tm', None, 'head'), may hold values from -6 to 6
- out_weight: bfloat16 [1024, 1024], P('head'), may hold values from -0.1875 to 0.1875
- out_grad: bfloat16 [16, 392, 1024], P('tm'), may hold values from -6 to 6
- clip_starts: int32 [16], P('tm'), may hold values from 0 to 1, as said below
Outputs:
- projected: bfloat16 [16, 392, 1024], P('tm', 'head')
- grad_queries: bfloat16 [16, 392, 1024], P('tm', None, 'head')
- grad_keys: bfloat16 [16, 392, 1024], P('tm', None, 'head')
- grad_values: bfloat16 [16, 392, 1024], P('tm', None, 'head')
The draws below stay inside these ranges and needn't reach their ends.
Inputs may be any that keep to these rules, and one draw needn't show every extreme that they name: `clip_starts`: the last 8 clips never begin a new video.
All inputs are finite; a program needn't handle non-finite values.
Results may differ from the reference program's by a relative error of at most 0.0087.
Values may be sent and summed in bfloat16 or wider, within the bound.
A program may use at most 64 MiB of HBM per device.

```python
import jax
import jax.numpy as jnp
from jax import lax

HEADS = 16
HEAD_DIM = 64
WIDTH = 1024
TOK = 392
POOL = 4
MEM = 8
CLIPS = 16


def base_field(key, seed_tag):
    return jax.random.truncated_normal(jax.random.fold_in(key, seed_tag), -6.0, 6.0, (CLIPS, TOK, WIDTH), jnp.float32)


def draw_queries(key, part):
    field = base_field(key, 1)
    return field.astype(jnp.bfloat16)


def draw_key_tokens(key, part):
    field = base_field(key, 2)
    return field.astype(jnp.bfloat16)


def draw_clip_starts(key, part):
    dice = jax.random.randint(jax.random.fold_in(key, 21), (CLIPS,), 0, 4)
    forced = jax.random.randint(jax.random.fold_in(key, 22), (), 0, CLIPS - MEM)
    positions = jnp.arange(CLIPS)
    starts = jnp.where((dice == 0) | (positions == forced), 1, 0).astype(jnp.int32)
    late = positions >= CLIPS - MEM
    return jnp.where(late, 0, starts).astype(jnp.int32)


def levels(own_key, shape, pieces, least, high):
    loudness = 1.0
    for dim, parts in pieces:
        steps = jax.random.uniform(jax.random.fold_in(jax.random.fold_in(own_key, 6), dim), (parts,), jnp.float32, least / len(pieces), high / len(pieces))
        loudness = loudness * jnp.repeat(jnp.exp(steps), shape[dim] // parts).reshape((-1,) + (1,) * (len(shape) - 1 - dim))
    return loudness


def noise(key, shape, deviation, reach, pieces=(), held_as=jnp.bfloat16):
    loudness = levels(key, shape, pieces, -0.22, 0.18) if pieces else 1.0
    result = jax.random.normal(key, shape, jnp.float32) * deviation * loudness
    return jnp.minimum(jnp.maximum(result, -reach), reach).astype(held_as)


def setup_inputs(seed: int = 0) -> dict:
    key_list = jax.random.split(jax.random.key(seed), 7)
    return {
        "queries": draw_queries(jax.random.fold_in(key_list[6], 71), 0),
        "key_tokens": draw_key_tokens(jax.random.fold_in(key_list[6], 71), 0),
        "value_tokens": noise(key_list[2], (CLIPS, TOK, WIDTH), 1.0, 6.0, ((0, 16), (2, 2))),
        "out_weight": noise(key_list[3], (WIDTH, WIDTH), WIDTH ** -0.5, 0.1875, ((0, 2),)),
        "out_grad": noise(key_list[4], (CLIPS, TOK, WIDTH), 1.0, 6.0, ((0, 16),)),
        "clip_starts": draw_clip_starts(jax.random.fold_in(key_list[6], 71), 0),
    }


def delayed(series, places):
    return jnp.concatenate([jnp.zeros((places,), series.dtype), series[:series.shape[0] - places]])


def clip_terms(query_clip, key_ext, value_ext, column_mask, grad_clip):
    scale = HEAD_DIM ** -0.5
    query_heads = query_clip.astype(jnp.float32).reshape(TOK, HEADS, HEAD_DIM)
    key_heads = key_ext.astype(jnp.float32).reshape(-1, HEADS, HEAD_DIM)
    value_heads = value_ext.astype(jnp.float32).reshape(-1, HEADS, HEAD_DIM)
    grad_heads = grad_clip.astype(jnp.float32).reshape(TOK, HEADS, HEAD_DIM)
    scores = jnp.einsum('qhd,khd->hqk', query_heads, key_heads) * scale
    scores = jnp.where(column_mask[None, None, :] > 0, scores, -1e30)
    peak = jnp.max(scores, axis=-1, keepdims=True)
    expo = jnp.exp(scores - peak)
    probs = expo / jnp.sum(expo, axis=-1, keepdims=True)
    weights = lax.optimization_barrier(probs.astype(jnp.bfloat16)).astype(jnp.float32)
    attended = jnp.einsum('hqk,khd->qhd', weights, value_heads).reshape(TOK, WIDTH).astype(jnp.bfloat16)
    grad_probs = jnp.einsum('qhd,khd->hqk', grad_heads, value_heads)
    delta = jnp.sum(probs * grad_probs, axis=-1, keepdims=True)
    grad_scores = (probs * (grad_probs - delta) * scale).astype(jnp.bfloat16)
    grad_scores = lax.optimization_barrier(grad_scores).astype(jnp.float32)
    grad_query = jnp.einsum('hqk,khd->qhd', grad_scores, key_heads).reshape(TOK, WIDTH).astype(jnp.bfloat16)
    grad_key = jnp.einsum('hqk,qhd->khd', grad_scores, query_heads).reshape(-1, WIDTH)
    grad_value = jnp.einsum('hqk,qhd->khd', weights, grad_heads).reshape(-1, WIDTH)
    return attended, grad_query, grad_key, grad_value


def reference(queries, key_tokens, value_tokens, out_weight, out_grad, clip_starts):
    clips = queries.shape[0]
    pooled_count = TOK // POOL
    pooled_keys = key_tokens.astype(jnp.float32).reshape(clips, pooled_count, POOL, WIDTH).mean(axis=2).astype(jnp.bfloat16)
    pooled_values = value_tokens.astype(jnp.float32).reshape(clips, pooled_count, POOL, WIDTH).mean(axis=2).astype(jnp.bfloat16)
    keep = (1 - clip_starts).astype(jnp.float32)
    present = jnp.ones((clips,), jnp.float32)
    running = keep
    allowed_list = []
    for distance in range(1, MEM + 1):
        allowed_list.append(running * delayed(present, distance))
        running = running * delayed(keep, distance)
    allowed = jnp.stack(allowed_list, axis=1)
    grad_attended = jnp.dot(out_grad.reshape(clips * TOK, WIDTH), out_weight.T, preferred_element_type=jnp.float32)
    grad_attended = grad_attended.astype(jnp.bfloat16).reshape(clips, TOK, WIDTH)
    sources = jnp.maximum(jnp.arange(clips)[:, None] - jnp.arange(1, MEM + 1)[None, :], 0).astype(jnp.int32)

    def per_clip(position):
        memory_keys = pooled_keys[sources[position]].reshape(MEM * pooled_count, WIDTH)
        memory_values = pooled_values[sources[position]].reshape(MEM * pooled_count, WIDTH)
        key_ext = jnp.concatenate([key_tokens[position], memory_keys], axis=0)
        value_ext = jnp.concatenate([value_tokens[position], memory_values], axis=0)
        column_mask = jnp.concatenate([jnp.ones((TOK,), jnp.float32), jnp.repeat(allowed[position], pooled_count)])
        return clip_terms(queries[position], key_ext, value_ext, column_mask, grad_attended[position])

    attended, grad_queries, grad_key_ext, grad_value_ext = lax.map(per_clip, jnp.arange(clips))
    memory_key_grads = grad_key_ext[:, TOK:].reshape(clips, MEM, pooled_count, WIDTH)
    memory_value_grads = grad_value_ext[:, TOK:].reshape(clips, MEM, pooled_count, WIDTH)
    returned_keys = jnp.zeros((clips, pooled_count, WIDTH), jnp.float32)
    returned_values = jnp.zeros((clips, pooled_count, WIDTH), jnp.float32)
    for distance in range(1, MEM + 1):
        padding = jnp.zeros((distance, pooled_count, WIDTH), jnp.float32)
        returned_keys = returned_keys + jnp.concatenate([memory_key_grads[distance:, distance - 1], padding], axis=0)
        returned_values = returned_values + jnp.concatenate([memory_value_grads[distance:, distance - 1], padding], axis=0)
    grad_keys = (grad_key_ext[:, :TOK] + jnp.repeat(returned_keys, POOL, axis=1) / POOL).astype(jnp.bfloat16)
    grad_values = (grad_value_ext[:, :TOK] + jnp.repeat(returned_values, POOL, axis=1) / POOL).astype(jnp.bfloat16)
    projected = jnp.dot(attended.reshape(clips * TOK, WIDTH), out_weight, preferred_element_type=jnp.float32)
    projected = projected.astype(jnp.bfloat16).reshape(clips, TOK, WIDTH)
    return projected, grad_queries, grad_keys, grad_values
```

```python
import functools

import jax
import jax.numpy as jnp
from jax import lax
from jax.experimental import pallas as pl
from jax.experimental.pallas import tpu as pltpu
from jax.sharding import PartitionSpec as P

HEAD_DIM = 64
POOL = 4
MEM = 8
LANES = 2 * HEAD_DIM
EXCLUDED = -1e30
F32 = jnp.float32
BF16 = jnp.bfloat16
BY_COLUMN = (((1,), (1,)), ((), ()))
BY_ROW = (((0,), (0,)), ((), ()))


def attention_kernel(
    flags, q_ref, k_ref, v_ref, mem_ref, weight_ref, grad_ref,
    partial_ref, dq_ref, own_ref, memory_grad_ref,
    key_ext, value_ext, bias,
):
    step = pl.program_id(0)
    tokens = q_ref.shape[0]
    pooled = mem_ref.shape[2]
    pitch = -(-pooled // 8) * 8
    base = MEM * pitch

    @pl.when(step == 0)
    def _():
        bias[...] = jnp.full(bias.shape, EXCLUDED, F32)
        key_ext[...] = jnp.zeros(key_ext.shape, F32)
        value_ext[...] = jnp.zeros(value_ext.shape, F32)
        for slot in range(MEM):
            level = jnp.where(flags[slot] > 0, 0.0, EXCLUDED).astype(F32)
            bias[slot * pitch : slot * pitch + pooled, :] = jnp.full((pooled, LANES), level, F32)
        bias[base : base + tokens, :] = jnp.zeros((tokens, LANES), F32)

    for slot in range(MEM):
        rows = slice(slot * pitch, slot * pitch + pooled)
        key_ext[rows, :] = mem_ref[slot, 0].astype(F32)
        value_ext[rows, :] = mem_ref[slot, 1].astype(F32)
    key_ext[base : base + tokens, :] = k_ref[...].astype(F32)
    value_ext[base : base + tokens, :] = v_ref[...].astype(F32)

    scale = HEAD_DIM ** (-0.5)
    grad = lax.dot_general(grad_ref[...], weight_ref[...], BY_COLUMN, preferred_element_type=F32)
    query = q_ref[...].astype(F32)
    keys = key_ext[...]
    values = value_ext[...]
    key_pair = keys.astype(BF16)
    token_lane = lax.broadcasted_iota(jnp.int32, (tokens, LANES), 1)
    ext_lane = lax.broadcasted_iota(jnp.int32, keys.shape, 1)
    attended, dq, dk, dv = [], [], [], []
    for side in range(2):
        mine = (token_lane < HEAD_DIM) if side == 0 else (token_lane >= HEAD_DIM)
        mine_ext = (ext_lane < HEAD_DIM) if side == 0 else (ext_lane >= HEAD_DIM)
        spare = HEAD_DIM * (1 - side)
        query_aug = jnp.where(mine, query, jnp.where(token_lane == spare, 1.0, 0.0)).astype(BF16)
        key_aug = jnp.where(mine_ext, keys, bias[...]).astype(BF16)
        value_aug = jnp.where(mine_ext, values, 1.0).astype(BF16)
        scores = lax.dot_general(query_aug, key_aug, BY_COLUMN, preferred_element_type=F32)
        peak = jnp.max(scores, axis=1, keepdims=True)
        expo = jnp.exp((scores - peak) * scale)
        expo_low = expo.astype(BF16)
        gathered = jnp.dot(expo_low, value_aug, preferred_element_type=F32)
        inverse = 1.0 / pltpu.roll(gathered, HEAD_DIM, 1)
        attended_side = jnp.where(mine, gathered * inverse, 0.0)
        grad_side = jnp.where(mine, grad * inverse, 0.0).astype(BF16)
        delta = jnp.sum(grad_side.astype(F32) * attended_side, axis=1, keepdims=True)
        high = delta.astype(BF16).astype(F32)
        low = delta - high
        grad_aug = jnp.where(
            mine,
            grad_side.astype(F32),
            jnp.where(token_lane == spare, -high, jnp.where(token_lane == spare + 1, -low, 0.0)),
        ).astype(BF16)
        centred = lax.dot_general(grad_aug, value_aug, BY_COLUMN, preferred_element_type=F32)
        grad_scores = (expo * centred).astype(BF16)
        query_side = jnp.where(mine, query * scale, 0.0).astype(BF16)
        dq.append(jnp.dot(grad_scores, key_pair, preferred_element_type=F32))
        dk.append(lax.dot_general(grad_scores, query_side, BY_ROW, preferred_element_type=F32))
        dv.append(lax.dot_general(expo_low, grad_side, BY_ROW, preferred_element_type=F32))
        attended.append(attended_side)
    dq_ref[...] = (jnp.where(token_lane < HEAD_DIM, dq[0], dq[1]) * scale).astype(BF16)
    for which, total in enumerate((dk[0] + dk[1], dv[0] + dv[1])):
        for slot in range(MEM):
            memory_grad_ref[slot, which] = total[slot * pitch : slot * pitch + pooled, :].astype(BF16)
        own_ref[which] = total[base : base + tokens, :]
    share = jnp.dot(
        (attended[0] + attended[1]).astype(BF16), weight_ref[...], preferred_element_type=F32
    )

    @pl.when(step == 0)
    def _():
        partial_ref[...] = share

    @pl.when(step > 0)
    def _():
        partial_ref[...] += share


def attention(flags, queries, keys, values, memory, weight, grad):
    tokens, width = queries.shape
    full = weight.shape[1]
    pooled = memory.shape[2]
    extent = MEM * (-(-pooled // 8) * 8) + tokens
    columns = pl.BlockSpec((tokens, LANES), lambda i: (0, i))
    memory_block = pl.BlockSpec((MEM, 2, pooled, LANES), lambda i: (0, 0, 0, i))
    return pl.pallas_call(
        attention_kernel,
        grid=(width // LANES,),
        in_specs=[
            pl.BlockSpec(memory_space=pltpu.SMEM),
            columns,
            columns,
            columns,
            memory_block,
            pl.BlockSpec((LANES, full), lambda i: (i, 0)),
            pl.BlockSpec((tokens, full), lambda i: (0, 0)),
        ],
        out_specs=[
            pl.BlockSpec((tokens, full), lambda i: (0, 0)),
            columns,
            pl.BlockSpec((2, tokens, LANES), lambda i: (0, 0, i)),
            memory_block,
        ],
        out_shape=[
            jax.ShapeDtypeStruct((tokens, full), F32),
            jax.ShapeDtypeStruct((tokens, width), BF16),
            jax.ShapeDtypeStruct((2, tokens, width), F32),
            jax.ShapeDtypeStruct((MEM, 2, pooled, width), BF16),
        ],
        scratch_shapes=[pltpu.VMEM((extent, LANES), F32)] * 3,
        compiler_params=pltpu.CompilerParams(dimension_semantics=("arbitrary",)),
        name="attention",
    )(flags, queries, keys, values, memory, weight, grad)


def passed_along(block, axis, distance):
    devices = range(lax.axis_size(axis))
    route = [(i - distance, i) for i in devices if i - distance in devices]
    return lax.ppermute(block, axis, route)


def local(queries, key_tokens, value_tokens, out_weight, out_grad, clip_starts):
    token_count, local_width = queries.shape[1:]
    pooled_count = token_count // POOL
    pooled_own = (
        jnp.stack([key_tokens[0], value_tokens[0]])
        .astype(F32)
        .reshape(2, pooled_count, POOL, local_width)
        .mean(axis=2)
        .astype(BF16)
    )
    starts = lax.all_gather(clip_starts.astype(F32), "tm", tiled=True)
    mine = lax.axis_index("tm")
    running = 1 - clip_starts[0].astype(F32)
    flags = []
    for distance in range(1, MEM + 1):
        earlier = mine - distance
        flags.append(jnp.where(earlier >= 0, running, 0.0))
        running = running * (1 - starts[jnp.maximum(earlier, 0)])
    memory = jnp.stack([passed_along(pooled_own, "tm", d) for d in range(1, MEM + 1)])
    partial, dq, own, memory_grads = attention(
        jnp.stack(flags).astype(jnp.int32),
        queries[0], key_tokens[0], value_tokens[0], memory, out_weight, out_grad[0],
    )
    projected = lax.psum_scatter(partial, "head", scatter_dimension=0, tiled=True).astype(BF16)
    returned = jnp.zeros((2, pooled_count, local_width), F32)
    for distance in range(1, MEM + 1):
        returned = returned + passed_along(memory_grads[distance - 1], "tm", -distance).astype(F32)
    both = (own + jnp.repeat(returned, POOL, axis=1) / POOL).astype(BF16)
    return (projected[None], dq[None], both[:1], both[1:])


def solution(mesh):
    return jax.shard_map(
        local,
        mesh=mesh,
        in_specs=(
            P("tm", None, "head"),
            P("tm", None, "head"),
            P("tm", None, "head"),
            P("head", None),
            P("tm", None, None),
            P("tm"),
        ),
        out_specs=(
            P("tm", "head", None),
            P("tm", None, "head"),
            P("tm", None, "head"),
            P("tm", None, "head"),
        ),
        check_vma=False,
    )
```

```python
import functools

import jax
import jax.numpy as jnp
from jax import lax
from jax.experimental import pallas as pl
from jax.experimental.pallas import tpu as pltpu
from jax.sharding import PartitionSpec as P

HEAD_DIM = 64
POOL = 4
MEM = 8
GROUP = 4
LANES = 2 * HEAD_DIM
EXCLUDED = -1e30
F32 = jnp.float32
BF16 = jnp.bfloat16
BY_COLUMN = (((1,), (1,)), ((), ()))
BY_ROW = (((0,), (0,)), ((), ()))


def attention_kernel(
    start, q_ref, k_ref, v_ref, mem_ref, weight_ref, grad_ref,
    share_ref, dq_ref, own_ref, memory_grad_ref,
    key_ext, value_ext, bias, partial_ref,
):
    step = pl.program_id(0)
    tokens = q_ref.shape[0]
    pooled = tokens // POOL
    pitch = mem_ref.shape[2]
    base = MEM * pitch

    @pl.when(step == 0)
    def _():
        bias[...] = jnp.full(bias.shape, EXCLUDED, F32)
        running = jnp.full((1, LANES), 1 - start[0], jnp.int32).astype(F32)
        for slot in range(MEM):
            keep = mem_ref[slot, 0, pooled : pooled + 1, :].astype(F32)
            exists = mem_ref[slot, 0, pooled + 1 : pooled + 2, :].astype(F32)
            level = (1.0 - running * exists) * EXCLUDED
            bias[slot * pitch : slot * pitch + pooled, :] = jnp.broadcast_to(level, (pooled, LANES))
            running = running * keep
        bias[base : base + tokens, :] = jnp.zeros((tokens, LANES), F32)

    for slot in range(MEM):
        rows = slice(slot * pitch, (slot + 1) * pitch)
        key_ext[rows, :] = mem_ref[slot, 0].astype(F32)
        value_ext[rows, :] = mem_ref[slot, 1].astype(F32)
    key_ext[base : base + tokens, :] = k_ref[...].astype(F32)
    value_ext[base : base + tokens, :] = v_ref[...].astype(F32)

    scale = HEAD_DIM ** (-0.5)
    grad = lax.dot_general(grad_ref[...], weight_ref[...], BY_COLUMN, preferred_element_type=F32)
    query = q_ref[...].astype(F32)
    keys = key_ext[...]
    values = value_ext[...]
    key_pair = keys.astype(BF16)
    token_lane = lax.broadcasted_iota(jnp.int32, (tokens, LANES), 1)
    ext_lane = lax.broadcasted_iota(jnp.int32, keys.shape, 1)
    attended, dq, dk, dv = [], [], [], []
    for side in range(2):
        mine = (token_lane < HEAD_DIM) if side == 0 else (token_lane >= HEAD_DIM)
        mine_ext = (ext_lane < HEAD_DIM) if side == 0 else (ext_lane >= HEAD_DIM)
        spare = HEAD_DIM * (1 - side)
        query_aug = jnp.where(mine, query, jnp.where(token_lane == spare, 1.0, 0.0)).astype(BF16)
        key_aug = jnp.where(mine_ext, keys, bias[...]).astype(BF16)
        value_aug = jnp.where(mine_ext, values, 1.0).astype(BF16)
        scores = lax.dot_general(query_aug, key_aug, BY_COLUMN, preferred_element_type=F32)
        peak = jnp.max(scores, axis=1, keepdims=True)
        expo = jnp.exp((scores - peak) * scale)
        expo_low = expo.astype(BF16)
        gathered = jnp.dot(expo_low, value_aug, preferred_element_type=F32)
        inverse = 1.0 / pltpu.roll(gathered, HEAD_DIM, 1)
        attended_side = jnp.where(mine, gathered * inverse, 0.0)
        grad_side = jnp.where(mine, grad * inverse, 0.0).astype(BF16)
        delta = jnp.sum(grad_side.astype(F32) * attended_side, axis=1, keepdims=True)
        high = delta.astype(BF16).astype(F32)
        low = delta - high
        grad_aug = jnp.where(
            mine,
            grad_side.astype(F32),
            jnp.where(token_lane == spare, -high, jnp.where(token_lane == spare + 1, -low, 0.0)),
        ).astype(BF16)
        centred = lax.dot_general(grad_aug, value_aug, BY_COLUMN, preferred_element_type=F32)
        grad_scores = (expo * centred).astype(BF16)
        query_side = jnp.where(mine, query * scale, 0.0).astype(BF16)
        dq.append(jnp.dot(grad_scores, key_pair, preferred_element_type=F32))
        dk.append(lax.dot_general(grad_scores, query_side, BY_ROW, preferred_element_type=F32))
        dv.append(lax.dot_general(expo_low, grad_side, BY_ROW, preferred_element_type=F32))
        attended.append(attended_side)
    dq_ref[...] = (jnp.where(token_lane < HEAD_DIM, dq[0], dq[1]) * scale).astype(BF16)
    for which, total in enumerate((dk[0] + dk[1], dv[0] + dv[1])):
        for slot in range(MEM):
            memory_grad_ref[slot, which] = total[slot * pitch : (slot + 1) * pitch, :].astype(BF16)
        own_ref[which] = total[base : base + tokens, :]
    share = jnp.dot(
        (attended[0] + attended[1]).astype(BF16), weight_ref[...], preferred_element_type=F32
    )

    @pl.when(step == 0)
    def _():
        partial_ref[...] = share

    @pl.when(step > 0)
    def _():
        partial_ref[...] += share

    @pl.when(step == pl.num_programs(0) - 1)
    def _():
        rows = share_ref.shape[1]
        for part in range(share_ref.shape[0]):
            share_ref[part] = partial_ref[part * rows : (part + 1) * rows, :].astype(BF16)


def attention(start, queries, keys, values, memory, weight, grad, parts):
    tokens, width = queries.shape
    full = weight.shape[1]
    pitch = memory.shape[2]
    extent = MEM * pitch + tokens
    columns = pl.BlockSpec((tokens, LANES), lambda i: (0, i))
    memory_block = pl.BlockSpec((MEM, 2, pitch, LANES), lambda i: (0, 0, 0, i))
    return pl.pallas_call(
        attention_kernel,
        grid=(width // LANES,),
        in_specs=[
            pl.BlockSpec(memory_space=pltpu.SMEM),
            columns,
            columns,
            columns,
            memory_block,
            pl.BlockSpec((LANES, full), lambda i: (i, 0)),
            pl.BlockSpec((tokens, full), lambda i: (0, 0)),
        ],
        out_specs=[
            pl.BlockSpec((parts, tokens // parts, full), lambda i: (0, 0, 0)),
            columns,
            pl.BlockSpec((2, tokens, LANES), lambda i: (0, 0, i)),
            memory_block,
        ],
        out_shape=[
            jax.ShapeDtypeStruct((parts, tokens // parts, full), BF16),
            jax.ShapeDtypeStruct((tokens, width), BF16),
            jax.ShapeDtypeStruct((2, tokens, width), F32),
            jax.ShapeDtypeStruct((MEM, 2, pitch, width), BF16),
        ],
        scratch_shapes=[pltpu.VMEM((extent, LANES), F32)] * 3 + [pltpu.VMEM((tokens, full), F32)],
        compiler_params=pltpu.CompilerParams(dimension_semantics=("arbitrary",)),
        name="attention",
    )(start, queries, keys, values, memory, weight, grad)


def remote(source, target, send, receive, device):
    return pltpu.make_async_remote_copy(
        src_ref=source,
        dst_ref=target,
        send_sem=send,
        recv_sem=receive,
        device_id=device,
        device_id_type=pl.DeviceIdType.MESH,
    )


def place(count):
    me = lax.axis_index("tm")
    core = lax.rem(me, 2)
    side = lax.rem(me // 2, 2)
    sibling = {"tm": me + 1 - 2 * core}
    across = {"tm": me + 2 - 4 * side}
    later = {"tm": lax.rem(me + GROUP, count)}
    earlier = {"tm": lax.rem(me + count - GROUP, count)}
    return me, core, side, sibling, across, later, earlier, me + GROUP < count, me >= GROUP


def greet(neighbours):
    barrier = pltpu.get_barrier_semaphore()
    for device in neighbours:
        pl.semaphore_signal(
            barrier, inc=1, device_id=device, device_id_type=pl.DeviceIdType.MESH
        )
    pl.semaphore_wait(barrier, len(neighbours))


def gather_kernel(count, start, k_ref, v_ref, out_ref, buf, send, receive, stored):
    me, core, side, sibling, across, later, earlier, has_later, has_earlier = place(count)
    tokens, width = k_ref.shape
    pooled = tokens // POOL
    pitch = out_ref.shape[2]
    row = lax.broadcasted_iota(jnp.int32, (pitch, tokens), 0)
    token = lax.broadcasted_iota(jnp.int32, (pitch, tokens), 1)
    inside = (token >= row * POOL) & (token < row * POOL + POOL)
    mixing = jnp.where(inside, 1.0 / POOL, 0.0).astype(BF16)
    line = lax.broadcasted_iota(jnp.int32, (pitch, width), 0)
    keep = jnp.full((pitch, width), 1 - start[0], jnp.int32).astype(F32)
    for which, ref in enumerate((k_ref, v_ref)):
        mean = jnp.dot(mixing, ref[...], preferred_element_type=F32)
        mean = jnp.where(line == pooled, keep, jnp.where(line == pooled + 1, 1.0, mean))
        buf[0, which] = mean.astype(BF16)

    @pl.when(jnp.logical_not(has_earlier))
    def _():
        for slot in (4, 8):
            buf[slot] = jnp.zeros(buf.shape[1:], BF16)

    greet([sibling, across, later, earlier])

    def move(source, target, which, number, device):
        return remote(
            buf.at[source, which], buf.at[target, which],
            send.at[number, which], receive.at[target, which], device,
        )

    def arrive(slot, which):
        move(slot, slot, which, 0, sibling).wait_recv()

    def store(slot, which):
        pltpu.make_async_copy(
            buf.at[slot, which], out_ref.at[slot - 1, which], stored.at[slot - 1, which]
        ).start()

    for which in range(2):
        pl.when(has_later)(lambda: move(0, 4, which, 0, later).start())
        pl.when(side == 0)(lambda: move(0, 2, which, 2, across).start())
        pl.when(core == 0)(lambda: move(0, 1, which, 4, sibling).start())
    for which in range(2):
        pl.when(has_earlier)(lambda: arrive(4, which))
        pl.when(has_later)(lambda: move(4, 8, which, 1, later).start())
        pl.when(side == 0)(lambda: move(4, 6, which, 3, across).start())
        pl.when(side == 1)(lambda: move(4, 2, which, 2, across).start())
        pl.when(core == 0)(lambda: move(4, 5, which, 5, sibling).start())
        pl.when(core == 1)(lambda: move(4, 3, which, 4, sibling).start())
        store(4, which)
    for which in range(2):
        arrive(2, which)
        pl.when(core == 0)(lambda: move(2, 3, which, 6, sibling).start())
        pl.when(core == 1)(lambda: move(2, 1, which, 6, sibling).start())
        store(2, which)
    for which in range(2):
        pl.when(has_earlier)(lambda: arrive(8, which))
        pl.when(side == 1)(lambda: move(8, 6, which, 3, across).start())
        pl.when(core == 1)(lambda: move(8, 7, which, 5, sibling).start())
        store(8, which)
    for which in range(2):
        arrive(6, which)
        pl.when(core == 0)(lambda: move(6, 7, which, 7, sibling).start())
        pl.when(core == 1)(lambda: move(6, 5, which, 7, sibling).start())
        store(6, which)
    for slot in (1, 3, 5, 7):
        for which in range(2):
            arrive(slot, which)
            store(slot, which)
    for which in range(2):
        for number in (0, 1):
            pl.when(has_later)(lambda: move(0, 4, which, number, later).wait_send())
        for number in range(2, 8):
            move(0, 2, which, number, across).wait_send()
        for slot in range(1, MEM + 1):
            pltpu.make_async_copy(
                buf.at[slot, which], out_ref.at[slot - 1, which], stored.at[slot - 1, which]
            ).wait()


def gather(start, keys, values, count):
    tokens, width = keys.shape
    pitch = -(-(tokens // POOL + 2) // 8) * 8
    whole = pl.BlockSpec(memory_space=pltpu.VMEM)
    return pl.pallas_call(
        functools.partial(gather_kernel, count),
        in_specs=[pl.BlockSpec(memory_space=pltpu.SMEM), whole, whole],
        out_specs=pl.BlockSpec(memory_space=pl.ANY),
        out_shape=jax.ShapeDtypeStruct((MEM, 2, pitch, width), BF16),
        scratch_shapes=[
            pltpu.VMEM((MEM + 1, 2, pitch, width), BF16),
            pltpu.SemaphoreType.DMA((8, 2)),
            pltpu.SemaphoreType.DMA((MEM + 1, 2)),
            pltpu.SemaphoreType.DMA((MEM, 2)),
        ],
        compiler_params=pltpu.CompilerParams(collective_id=1, has_side_effects=True),
        name="gather",
    )(start, keys, values)


def giving_kernel(
    count, parts, grads, own_ref, share_ref, projected_ref, dk_ref, dv_ref,
    landed, sums, shares, send, receive, share_send, share_receive,
):
    me, core, side, sibling, across, later, earlier, has_later, has_earlier = place(count)
    head = lax.axis_index("head")
    tokens = own_ref.shape[1]
    pitch = grads.shape[2]

    @pl.when(jnp.logical_not(has_later))
    def _():
        for number in (6, 7):
            landed[number] = jnp.zeros(landed.shape[1:], BF16)

    peers = [{"head": lax.rem(head + k, parts)} for k in range(1, parts)]
    greet([sibling, across, later, earlier] + peers)

    def move(source, number, which, device):
        return remote(
            source, landed.at[number, which],
            send.at[number, which], receive.at[number, which], device,
        )

    def slot(index, which):
        return grads.at[index - 1, which]

    for which in range(2):
        for number, bottom, step in ((3, 5, 2), (1, 7, -2), (2, 1, 2), (0, 3, -2)):
            move(slot(bottom + step * core, which), number, which, sibling).start()
    exchanges = []
    for k, peer in enumerate(peers):
        copy = remote(
            share_ref.at[lax.rem(head + k + 1, parts)], shares.at[k],
            share_send.at[k], share_receive.at[k], peer,
        )
        copy.start()
        exchanges.append(copy)

    def arrive(number, which):
        move(slot(1, which), number, which, sibling).wait_recv()
        return landed[number, which].astype(F32)

    is_core = core.astype(F32)
    is_side = side.astype(F32)
    for which in range(2):
        sums[1, which] = (grads[5, which].astype(F32) + arrive(3, which)).astype(BF16)
        move(sums.at[1, which], 5, which, across).start()
    for which in range(2):
        from_core = arrive(1, which)
        sums[0, which] = (grads[1, which].astype(F32) + arrive(2, which)).astype(BF16)
        move(sums.at[0, which], 4, which, across).start()
    for which in range(2):
        total = grads[7, which].astype(F32) + is_core * landed[1, which].astype(F32)
        total = total + is_side * arrive(5, which)
        sums[3, which] = total.astype(BF16)
        pl.when(has_earlier)(lambda: move(sums.at[3, which], 7, which, earlier).start())
    for which in range(2):
        total = grads[3, which].astype(F32) + (1 - is_core) * landed[1, which].astype(F32)
        total = total + is_core * arrive(0, which)
        total = total + (1 - is_side) * landed[5, which].astype(F32)
        total = total + is_side * arrive(4, which)
        pl.when(has_later)(
            lambda: move(slot(1, which), 7, which, sibling).wait_recv()
        )
        total = total + landed[7, which].astype(F32)
        sums[2, which] = total.astype(BF16)
        pl.when(has_earlier)(lambda: move(sums.at[2, which], 6, which, earlier).start())

    for copy in exchanges:
        copy.wait()
    projected = share_ref[head].astype(F32)
    for k in range(parts - 1):
        projected = projected + shares[k].astype(F32)
    projected_ref[...] = projected.astype(BF16)

    token = lax.broadcasted_iota(jnp.int32, (tokens, pitch), 0)
    row = lax.broadcasted_iota(jnp.int32, (tokens, pitch), 1)
    inside = (token >= row * POOL) & (token < row * POOL + POOL)
    spread = jnp.where(inside, 1.0 / POOL, 0.0).astype(BF16)
    for which, ref in enumerate((dk_ref, dv_ref)):
        pl.when(has_later)(
            lambda: move(slot(1, which), 6, which, sibling).wait_recv()
        )
        total = (1 - is_core) * landed[0, which].astype(F32) + landed[6, which].astype(F32)
        total = total + (1 - is_side) * landed[4, which].astype(F32)
        shared = jnp.dot(spread, total.astype(BF16), preferred_element_type=F32)
        ref[...] = (own_ref[which] + shared).astype(BF16)
    for which in range(2):
        for number in range(6):
            move(slot(1, which), number, which, sibling).wait_send()
        for number in (6, 7):
            pl.when(has_earlier)(
                lambda: move(slot(1, which), number, which, sibling).wait_send()
            )


def give_back(grads, own, share, count):
    _, tokens, width = own.shape
    parts, rows, full = share.shape
    pitch = grads.shape[2]
    whole = pl.BlockSpec(memory_space=pltpu.VMEM)
    return pl.pallas_call(
        functools.partial(giving_kernel, count, parts),
        in_specs=[whole] * 3,
        out_specs=[whole] * 3,
        out_shape=[
            jax.ShapeDtypeStruct((rows, full), BF16),
            jax.ShapeDtypeStruct((tokens, width), BF16),
            jax.ShapeDtypeStruct((tokens, width), BF16),
        ],
        scratch_shapes=[
            pltpu.VMEM((8, 2, pitch, width), BF16),
            pltpu.VMEM((4, 2, pitch, width), BF16),
            pltpu.VMEM((parts - 1, rows, full), BF16),
            pltpu.SemaphoreType.DMA((8, 2)),
            pltpu.SemaphoreType.DMA((8, 2)),
            pltpu.SemaphoreType.DMA((parts - 1,)),
            pltpu.SemaphoreType.DMA((parts - 1,)),
        ],
        compiler_params=pltpu.CompilerParams(collective_id=2, has_side_effects=True),
        name="give_back",
    )(grads, own, share)


def local(queries, key_tokens, value_tokens, out_weight, out_grad, clip_starts):
    count = lax.axis_size("tm")
    memory = gather(clip_starts, key_tokens[0], value_tokens[0], count)
    share, dq, own, memory_grads = attention(
        clip_starts, queries[0], key_tokens[0], value_tokens[0], memory, out_weight, out_grad[0],
        lax.axis_size("head"),
    )
    projected, dk, dv = give_back(memory_grads, own, share, count)
    return (projected[None], dq[None], dk[None], dv[None])


def solution(mesh):
    return jax.shard_map(
        local,
        mesh=mesh,
        in_specs=(
            P("tm", None, "head"),
            P("tm", None, "head"),
            P("tm", None, "head"),
            P("head", None),
            P("tm", None, None),
            P("tm"),
        ),
        out_specs=(
            P("tm", "head", None),
            P("tm", None, "head"),
            P("tm", None, "head"),
            P("tm", None, "head"),
        ),
        check_vma=False,
    )
```

```python
import functools

import jax
import jax.numpy as jnp
from jax import lax
from jax.experimental import pallas as pl
from jax.experimental.pallas import tpu as pltpu
from jax.sharding import PartitionSpec as P

HEAD_DIM = 64
POOL = 4
MEM = 8
GROUP = 4
LANES = 2 * HEAD_DIM
EXCLUDED = -1e30
F32 = jnp.float32
BF16 = jnp.bfloat16
BY_COLUMN = (((1,), (1,)), ((), ()))
BY_ROW = (((0,), (0,)), ((), ()))


def attention_kernel(
    start, q_ref, k_ref, v_ref, mem_ref, weight_ref, grad_ref,
    share_ref, dq_ref, own_ref, memory_grad_ref,
    key_ext, value_ext, bias, partial_ref,
):
    step = pl.program_id(0)
    tokens = q_ref.shape[0]
    pooled = tokens // POOL
    pitch = mem_ref.shape[2]
    base = MEM * pitch

    @pl.when(step == 0)
    def _():
        bias[...] = jnp.full(bias.shape, EXCLUDED, F32)
        running = jnp.full((1, LANES), 1 - start[0], jnp.int32).astype(F32)
        for slot in range(MEM):
            keep = mem_ref[slot, 0, pooled : pooled + 1, :].astype(F32)
            exists = mem_ref[slot, 0, pooled + 1 : pooled + 2, :].astype(F32)
            level = (1.0 - running * exists) * EXCLUDED
            bias[slot * pitch : slot * pitch + pooled, :] = jnp.broadcast_to(level, (pooled, LANES))
            running = running * keep
        bias[base : base + tokens, :] = jnp.zeros((tokens, LANES), F32)

    for slot in range(MEM):
        rows = slice(slot * pitch, (slot + 1) * pitch)
        key_ext[rows, :] = mem_ref[slot, 0].astype(F32)
        value_ext[rows, :] = mem_ref[slot, 1].astype(F32)
    key_ext[base : base + tokens, :] = k_ref[...].astype(F32)
    value_ext[base : base + tokens, :] = v_ref[...].astype(F32)

    scale = HEAD_DIM ** (-0.5)
    grad = lax.dot_general(grad_ref[...], weight_ref[...], BY_COLUMN, preferred_element_type=F32)
    query = q_ref[...].astype(F32)
    keys = key_ext[...]
    values = value_ext[...]
    key_pair = keys.astype(BF16)
    token_lane = lax.broadcasted_iota(jnp.int32, (tokens, LANES), 1)
    ext_lane = lax.broadcasted_iota(jnp.int32, keys.shape, 1)
    attended, dq, dk, dv = [], [], [], []
    for side in range(2):
        mine = (token_lane < HEAD_DIM) if side == 0 else (token_lane >= HEAD_DIM)
        mine_ext = (ext_lane < HEAD_DIM) if side == 0 else (ext_lane >= HEAD_DIM)
        spare = HEAD_DIM * (1 - side)
        query_aug = jnp.where(mine, query, jnp.where(token_lane == spare, 1.0, 0.0)).astype(BF16)
        key_aug = jnp.where(mine_ext, keys, bias[...]).astype(BF16)
        value_aug = jnp.where(mine_ext, values, 1.0).astype(BF16)
        scores = lax.dot_general(query_aug, key_aug, BY_COLUMN, preferred_element_type=F32)
        peak = jnp.max(scores, axis=1, keepdims=True)
        expo = jnp.exp((scores - peak) * scale)
        expo_low = expo.astype(BF16)
        gathered = jnp.dot(expo_low, value_aug, preferred_element_type=F32)
        inverse = 1.0 / pltpu.roll(gathered, HEAD_DIM, 1)
        attended_side = jnp.where(mine, gathered * inverse, 0.0)
        grad_side = jnp.where(mine, grad * inverse, 0.0).astype(BF16)
        delta = jnp.sum(grad_side.astype(F32) * attended_side, axis=1, keepdims=True)
        high = delta.astype(BF16).astype(F32)
        low = delta - high
        grad_aug = jnp.where(
            mine,
            grad_side.astype(F32),
            jnp.where(token_lane == spare, -high, jnp.where(token_lane == spare + 1, -low, 0.0)),
        ).astype(BF16)
        centred = lax.dot_general(grad_aug, value_aug, BY_COLUMN, preferred_element_type=F32)
        grad_scores = (expo * centred).astype(BF16)
        query_side = jnp.where(mine, query * scale, 0.0).astype(BF16)
        dq.append(jnp.dot(grad_scores, key_pair, preferred_element_type=F32))
        dk.append(lax.dot_general(grad_scores, query_side, BY_ROW, preferred_element_type=F32))
        dv.append(lax.dot_general(expo_low, grad_side, BY_ROW, preferred_element_type=F32))
        attended.append(attended_side)
    dq_ref[...] = (jnp.where(token_lane < HEAD_DIM, dq[0], dq[1]) * scale).astype(BF16)
    for which, total in enumerate((dk[0] + dk[1], dv[0] + dv[1])):
        for slot in range(MEM):
            memory_grad_ref[slot, which] = total[slot * pitch : (slot + 1) * pitch, :].astype(BF16)
        own_ref[which] = total[base : base + tokens, :]
    share = jnp.dot(
        (attended[0] + attended[1]).astype(BF16), weight_ref[...], preferred_element_type=F32
    )

    @pl.when(step == 0)
    def _():
        partial_ref[...] = share

    @pl.when(step > 0)
    def _():
        partial_ref[...] += share

    @pl.when(step == pl.num_programs(0) - 1)
    def _():
        rows = share_ref.shape[1]
        for part in range(share_ref.shape[0]):
            share_ref[part] = partial_ref[part * rows : (part + 1) * rows, :].astype(BF16)


def attention(start, queries, keys, values, memory, weight, grad, parts):
    tokens, width = queries.shape
    full = weight.shape[1]
    pitch = memory.shape[2]
    extent = MEM * pitch + tokens
    columns = pl.BlockSpec((tokens, LANES), lambda i: (0, i))
    memory_block = pl.BlockSpec((MEM, 2, pitch, LANES), lambda i: (0, 0, 0, i))
    return pl.pallas_call(
        attention_kernel,
        grid=(width // LANES,),
        in_specs=[
            pl.BlockSpec(memory_space=pltpu.SMEM),
            columns,
            columns,
            columns,
            memory_block,
            pl.BlockSpec((LANES, full), lambda i: (i, 0)),
            pl.BlockSpec((tokens, full), lambda i: (0, 0)),
        ],
        out_specs=[
            pl.BlockSpec((parts, tokens // parts, full), lambda i: (0, 0, 0)),
            columns,
            pl.BlockSpec((2, tokens, LANES), lambda i: (0, 0, i)),
            memory_block,
        ],
        out_shape=[
            jax.ShapeDtypeStruct((parts, tokens // parts, full), BF16),
            jax.ShapeDtypeStruct((tokens, width), BF16),
            jax.ShapeDtypeStruct((2, tokens, width), F32),
            jax.ShapeDtypeStruct((MEM, 2, pitch, width), BF16),
        ],
        scratch_shapes=[pltpu.VMEM((extent, LANES), F32)] * 3 + [pltpu.VMEM((tokens, full), F32)],
        compiler_params=pltpu.CompilerParams(dimension_semantics=("arbitrary",)),
        name="attention",
    )(start, queries, keys, values, memory, weight, grad)


def remote(source, target, send, receive, device):
    return pltpu.make_async_remote_copy(
        src_ref=source,
        dst_ref=target,
        send_sem=send,
        recv_sem=receive,
        device_id=device,
        device_id_type=pl.DeviceIdType.MESH,
    )


def place(count):
    me = lax.axis_index("tm")
    core = lax.rem(me, 2)
    side = lax.rem(me // 2, 2)
    sibling = {"tm": me + 1 - 2 * core}
    across = {"tm": me + 2 - 4 * side}
    later = {"tm": lax.rem(me + GROUP, count)}
    earlier = {"tm": lax.rem(me + count - GROUP, count)}
    return me, core, side, sibling, across, later, earlier, me + GROUP < count, me >= GROUP


def greet(neighbours):
    barrier = pltpu.get_barrier_semaphore()
    for device in neighbours:
        pl.semaphore_signal(
            barrier, inc=1, device_id=device, device_id_type=pl.DeviceIdType.MESH
        )
    pl.semaphore_wait(barrier, len(neighbours))


def gather_kernel(count, start, k_ref, v_ref, out_ref, buf, send, receive, stored):
    me, core, side, sibling, across, later, earlier, has_later, has_earlier = place(count)
    tokens, width = k_ref.shape
    pooled = tokens // POOL
    pitch = out_ref.shape[2]
    row = lax.broadcasted_iota(jnp.int32, (pitch, tokens), 0)
    token = lax.broadcasted_iota(jnp.int32, (pitch, tokens), 1)
    inside = (token >= row * POOL) & (token < row * POOL + POOL)
    mixing = jnp.where(inside, 1.0 / POOL, 0.0).astype(BF16)
    line = lax.broadcasted_iota(jnp.int32, (pitch, width), 0)
    keep = jnp.full((pitch, width), 1 - start[0], jnp.int32).astype(F32)
    for which, ref in enumerate((k_ref, v_ref)):
        mean = jnp.dot(mixing, ref[...], preferred_element_type=F32)
        mean = jnp.where(line == pooled, keep, jnp.where(line == pooled + 1, 1.0, mean))
        buf[0, which] = mean.astype(BF16)

    @pl.when(jnp.logical_not(has_earlier))
    def _():
        for slot in (4, 8):
            buf[slot] = jnp.zeros(buf.shape[1:], BF16)

    greet([sibling, across, later, earlier])

    def move(source, target, which, number, device):
        return remote(
            buf.at[source, which], buf.at[target, which],
            send.at[number, which], receive.at[target, which], device,
        )

    def arrive(slot, which):
        move(slot, slot, which, 0, sibling).wait_recv()

    def store(slot, which):
        pltpu.make_async_copy(
            buf.at[slot, which], out_ref.at[slot - 1, which], stored.at[slot - 1, which]
        ).start()

    for which in range(2):
        pl.when(has_later)(lambda: move(0, 4, which, 0, later).start())
        pl.when(side == 0)(lambda: move(0, 2, which, 2, across).start())
        pl.when(core == 0)(lambda: move(0, 1, which, 4, sibling).start())
    for which in range(2):
        pl.when(has_earlier)(lambda: arrive(4, which))
        pl.when(has_later)(lambda: move(4, 8, which, 1, later).start())
        pl.when(side == 0)(lambda: move(4, 6, which, 3, across).start())
        pl.when(side == 1)(lambda: move(4, 2, which, 2, across).start())
        pl.when(core == 0)(lambda: move(4, 5, which, 5, sibling).start())
        pl.when(core == 1)(lambda: move(4, 3, which, 4, sibling).start())
        store(4, which)
    for which in range(2):
        arrive(2, which)
        pl.when(core == 0)(lambda: move(2, 3, which, 6, sibling).start())
        pl.when(core == 1)(lambda: move(2, 1, which, 6, sibling).start())
        store(2, which)
    for which in range(2):
        pl.when(has_earlier)(lambda: arrive(8, which))
        pl.when(side == 1)(lambda: move(8, 6, which, 3, across).start())
        pl.when(core == 1)(lambda: move(8, 7, which, 5, sibling).start())
        store(8, which)
    for which in range(2):
        arrive(6, which)
        pl.when(core == 0)(lambda: move(6, 7, which, 7, sibling).start())
        pl.when(core == 1)(lambda: move(6, 5, which, 7, sibling).start())
        store(6, which)
    for slot in (1, 3, 5, 7):
        for which in range(2):
            arrive(slot, which)
            store(slot, which)
    for which in range(2):
        for number in (0, 1):
            pl.when(has_later)(lambda: move(0, 4, which, number, later).wait_send())
        for number in range(2, 8):
            move(0, 2, which, number, across).wait_send()
        for slot in range(1, MEM + 1):
            pltpu.make_async_copy(
                buf.at[slot, which], out_ref.at[slot - 1, which], stored.at[slot - 1, which]
            ).wait()


def gather(start, keys, values, count):
    tokens, width = keys.shape
    pitch = -(-(tokens // POOL + 2) // 8) * 8
    whole = pl.BlockSpec(memory_space=pltpu.VMEM)
    return pl.pallas_call(
        functools.partial(gather_kernel, count),
        in_specs=[pl.BlockSpec(memory_space=pltpu.SMEM), whole, whole],
        out_specs=pl.BlockSpec(memory_space=pl.ANY),
        out_shape=jax.ShapeDtypeStruct((MEM, 2, pitch, width), BF16),
        scratch_shapes=[
            pltpu.VMEM((MEM + 1, 2, pitch, width), BF16),
            pltpu.SemaphoreType.DMA((8, 2)),
            pltpu.SemaphoreType.DMA((MEM + 1, 2)),
            pltpu.SemaphoreType.DMA((MEM, 2)),
        ],
        compiler_params=pltpu.CompilerParams(collective_id=1, has_side_effects=True),
        name="gather",
    )(start, keys, values)


def giving_kernel(
    count, parts, grads, share_ref, projected_ref, returned_ref,
    landed, sums, shares, send, receive, share_send, share_receive,
):
    me, core, side, sibling, across, later, earlier, has_later, has_earlier = place(count)
    head = lax.axis_index("head")

    @pl.when(jnp.logical_not(has_later))
    def _():
        for number in (6, 7):
            landed[number] = jnp.zeros(landed.shape[1:], BF16)

    peers = [{"head": lax.rem(head + k, parts)} for k in range(1, parts)]
    greet([sibling, across, later, earlier] + peers)

    def move(source, number, which, device):
        return remote(
            source, landed.at[number, which],
            send.at[number, which], receive.at[number, which], device,
        )

    def slot(index, which):
        return grads.at[index - 1, which]

    for which in range(2):
        for number, bottom, step in ((3, 5, 2), (1, 7, -2), (2, 1, 2), (0, 3, -2)):
            move(slot(bottom + step * core, which), number, which, sibling).start()
    exchanges = []
    for k, peer in enumerate(peers):
        copy = remote(
            share_ref.at[lax.rem(head + k + 1, parts)], shares.at[k],
            share_send.at[k], share_receive.at[k], peer,
        )
        copy.start()
        exchanges.append(copy)

    def arrive(number, which):
        move(slot(1, which), number, which, sibling).wait_recv()
        return landed[number, which].astype(F32)

    is_core = core.astype(F32)
    is_side = side.astype(F32)
    for which in range(2):
        sums[1, which] = (grads[5, which].astype(F32) + arrive(3, which)).astype(BF16)
        move(sums.at[1, which], 5, which, across).start()
    for which in range(2):
        from_core = arrive(1, which)
        sums[0, which] = (grads[1, which].astype(F32) + arrive(2, which)).astype(BF16)
        move(sums.at[0, which], 4, which, across).start()
    for which in range(2):
        total = grads[7, which].astype(F32) + is_core * landed[1, which].astype(F32)
        total = total + is_side * arrive(5, which)
        sums[3, which] = total.astype(BF16)
        pl.when(has_earlier)(lambda: move(sums.at[3, which], 7, which, earlier).start())
    for which in range(2):
        total = grads[3, which].astype(F32) + (1 - is_core) * landed[1, which].astype(F32)
        total = total + is_core * arrive(0, which)
        total = total + (1 - is_side) * landed[5, which].astype(F32)
        total = total + is_side * arrive(4, which)
        pl.when(has_later)(
            lambda: move(slot(1, which), 7, which, sibling).wait_recv()
        )
        total = total + landed[7, which].astype(F32)
        sums[2, which] = total.astype(BF16)
        pl.when(has_earlier)(lambda: move(sums.at[2, which], 6, which, earlier).start())

    for copy in exchanges:
        copy.wait()
    projected = share_ref[head].astype(F32)
    for k in range(parts - 1):
        projected = projected + shares[k].astype(F32)
    projected_ref[...] = projected.astype(BF16)

    for which in range(2):
        pl.when(has_later)(
            lambda: move(slot(1, which), 6, which, sibling).wait_recv()
        )
        total = (1 - is_core) * landed[0, which].astype(F32) + landed[6, which].astype(F32)
        total = total + (1 - is_side) * landed[4, which].astype(F32)
        returned_ref[which] = total.astype(BF16)
    for which in range(2):
        for number in range(6):
            move(slot(1, which), number, which, sibling).wait_send()
        for number in (6, 7):
            pl.when(has_earlier)(
                lambda: move(slot(1, which), number, which, sibling).wait_send()
            )


def give_back(grads, share, count):
    parts, rows, full = share.shape
    pitch, width = grads.shape[2:]
    whole = pl.BlockSpec(memory_space=pltpu.VMEM)
    return pl.pallas_call(
        functools.partial(giving_kernel, count, parts),
        in_specs=[whole] * 2,
        out_specs=[whole] * 2,
        out_shape=[
            jax.ShapeDtypeStruct((rows, full), BF16),
            jax.ShapeDtypeStruct((2, pitch, width), BF16),
        ],
        scratch_shapes=[
            pltpu.VMEM((8, 2, pitch, width), BF16),
            pltpu.VMEM((4, 2, pitch, width), BF16),
            pltpu.VMEM((parts - 1, rows, full), BF16),
            pltpu.SemaphoreType.DMA((8, 2)),
            pltpu.SemaphoreType.DMA((8, 2)),
            pltpu.SemaphoreType.DMA((parts - 1,)),
            pltpu.SemaphoreType.DMA((parts - 1,)),
        ],
        compiler_params=pltpu.CompilerParams(collective_id=2, has_side_effects=True),
        name="give_back",
    )(grads, share)


def finish_kernel(own_ref, returned_ref, share_ref, projected_ref, dk_ref, dv_ref):
    tokens = own_ref.shape[1]
    pitch = returned_ref.shape[1]
    token = lax.broadcasted_iota(jnp.int32, (tokens, pitch), 0)
    row = lax.broadcasted_iota(jnp.int32, (tokens, pitch), 1)
    inside = (token >= row * POOL) & (token < row * POOL + POOL)
    spread = jnp.where(inside, 1.0 / POOL, 0.0).astype(BF16)
    for which, ref in enumerate((dk_ref, dv_ref)):
        shared = jnp.dot(spread, returned_ref[which], preferred_element_type=F32)
        ref[...] = (own_ref[which] + shared).astype(BF16)
    projected_ref[...] = share_ref[...]


def finish(own, returned, share):
    _, tokens, width = own.shape
    pitch = returned.shape[1]
    rows, full = share.shape
    steps = width // LANES
    columns = pl.BlockSpec((tokens, LANES), lambda i: (0, i))
    shares = pl.BlockSpec((rows, full // steps), lambda i: (0, i))
    return pl.pallas_call(
        finish_kernel,
        grid=(steps,),
        in_specs=[
            pl.BlockSpec((2, tokens, LANES), lambda i: (0, 0, i)),
            pl.BlockSpec((2, pitch, LANES), lambda i: (0, 0, i)),
            shares,
        ],
        out_specs=[shares, columns, columns],
        out_shape=[
            jax.ShapeDtypeStruct((rows, full), BF16),
            jax.ShapeDtypeStruct((tokens, width), BF16),
            jax.ShapeDtypeStruct((tokens, width), BF16),
        ],
        compiler_params=pltpu.CompilerParams(dimension_semantics=("arbitrary",)),
        name="finish",
    )(own, returned, share)


def local(queries, key_tokens, value_tokens, out_weight, out_grad, clip_starts):
    count = lax.axis_size("tm")
    memory = gather(clip_starts, key_tokens[0], value_tokens[0], count)
    share, dq, own, memory_grads = attention(
        clip_starts, queries[0], key_tokens[0], value_tokens[0], memory, out_weight, out_grad[0],
        lax.axis_size("head"),
    )
    share, returned = give_back(memory_grads, share, count)
    projected, dk, dv = finish(own, returned, share)
    return (projected[None], dq[None], dk[None], dv[None])


def solution(mesh):
    return jax.shard_map(
        local,
        mesh=mesh,
        in_specs=(
            P("tm", None, "head"),
            P("tm", None, "head"),
            P("tm", None, "head"),
            P("head", None),
            P("tm", None, None),
            P("tm"),
        ),
        out_specs=(
            P("tm", "head", None),
            P("tm", None, "head"),
            P("tm", None, "head"),
            P("tm", None, "head"),
        ),
        check_vma=False,
    )
```
